32 devices in a mesh: gx: 16 (over z, y, x), gy: 2 (over core).
Axes of the slice: x: 2, y: 2, z: 4, core: 2. Of those that a mesh axis runs over, the one named last changes fastest.
Arguments:
- features: bfloat16 [16, 2, 2, 512, 128], P('gx', 'gy'), may hold values from -6 to 6
- cotangent: bfloat16 [16, 2, 2, 512, 128], P('gx', 'gy'), may hold values from -6 to 6
- neighbours: int32 [16, 2, 2, 27], P('gx', 'gy'), may hold values from -1 to 17, as said below
- weights: bfloat16 [27, 128, 128], replicated, may hold values from -0.109375 to 0.109375
- channel_gain: float32 [128], replicated, may hold values from 0.5 to 2
Outputs:
- output: bfloat16 [16, 2, 2, 512, 128], P('gx', 'gy')
- input_grad: bfloat16 [16, 2, 2, 512, 128], P('gx', 'gy')
- weight_grad: float32 [27, 128, 128], replicated
- gain_grad: float32 [128], replicated
The draws below stay inside these ranges and needn't reach their ends.
Inputs may be any that keep to these rules, and one draw needn't show every extreme that they name: `neighbours`: entry [i, j, s, k] names, for slot s of device (i, j) and direction k = 9 (a + 1) + 3 (b + 1) + (c + 1), the block at block offset (a, b, c): the code (3 (i2 - i + 1) + (j2 - j + 1)) * 2 + s2 for slot s2 of device (i2, j2), always equal or beside (i, j), with i2 - i equal to 0 or a and j2 - j equal to 0 or b, or -1 where no occupied block lies. Codes are therefore at most 17. Entry 13 is 8 + s for an occupied slot; an empty slot has -1 everywhere. The relation is symmetric: the block named in direction k names the first one back in direction 26 - k. Some device has all 2 slots occupied.
All inputs are finite; a program needn't handle non-finite values.
Results may differ from the reference program's by a relative error of at most 0.0042.
Values may be sent and summed in bfloat16 or wider, within the bound.
A program may use at most 64 MiB of HBM per device.

```python
import math
import jax
import jax.numpy as jnp
from jax import lax

C = 128
VOXELS = 512
CAP = 2
GRID_X = 16
GRID_Y = 2


def draw_neighbours(key, part):
    positions = 4 * CAP
    devices = GRID_X * GRID_Y
    base = jax.random.fold_in(key, 7)
    order_key, count_key, full_key = jax.random.split(base, 3)
    device_keys = jax.random.split(order_key, devices)
    position_order = jax.vmap(lambda single: jax.random.permutation(single, positions))(device_keys).astype(jnp.int32)
    occupied_count = jax.random.randint(count_key, (devices,), max(1, CAP // 4), CAP + 1).astype(jnp.int32)
    full_device = jax.random.randint(full_key, (), 0, devices).astype(jnp.int32)
    device_ids = jnp.arange(devices, dtype=jnp.int32)
    occupied_count = jnp.where(device_ids == full_device, CAP, occupied_count)
    ranking = jnp.argsort(position_order, axis=1).astype(jnp.int32)
    slot_of_position = jnp.where(ranking < occupied_count[:, None], ranking, -1)
    world_slots = slot_of_position.reshape(GRID_X, GRID_Y, 2, 2, CAP).transpose(0, 2, 1, 3, 4)
    world_slots = world_slots.reshape(2 * GRID_X, 2 * GRID_Y, CAP)
    world_slots = jnp.pad(world_slots, 1, constant_values=-1)
    chosen = position_order[:, :CAP]
    slot_ids = jnp.arange(CAP, dtype=jnp.int32)
    present = slot_ids[None, :] < occupied_count[:, None]
    pos_x = chosen // (2 * CAP)
    pos_y = chosen // CAP % 2
    pos_z = chosen % CAP
    row_index = (device_ids // GRID_Y)[:, None]
    col_index = (device_ids % GRID_Y)[:, None]
    world_x = 2 * row_index + pos_x
    world_y = 2 * col_index + pos_y
    offsets = jnp.array([(a, b, c) for a in (-1, 0, 1) for b in (-1, 0, 1) for c in (-1, 0, 1)], dtype=jnp.int32)
    step_x = offsets[:, 0][None, None, :]
    step_y = offsets[:, 1][None, None, :]
    step_z = offsets[:, 2][None, None, :]
    target_x = world_x[:, :, None] + step_x
    target_y = world_y[:, :, None] + step_y
    target_z = pos_z[:, :, None] + step_z
    found = world_slots[target_x + 1, target_y + 1, target_z + 1]
    owner_x = jnp.floor_divide(target_x, 2)
    owner_y = jnp.floor_divide(target_y, 2)
    direction = (owner_x - row_index[:, :, None] + 1) * 3 + (owner_y - col_index[:, :, None] + 1)
    code_value = direction * CAP + found
    code_value = jnp.where((found >= 0) & present[:, :, None], code_value, -1)
    return code_value.reshape(GRID_X, GRID_Y, CAP, 27).astype(jnp.int32)


def steps_of(stream_key, extent, shards, least, high):
    gain = 1.0
    for position, blocks in shards:
        heights = jax.random.uniform(jax.random.fold_in(jax.random.fold_in(stream_key, 6), position), (blocks,), jnp.float32, least / len(shards), high / len(shards))
        gain = gain * jnp.repeat(jnp.exp(heights), extent[position] // blocks).reshape((-1,) + (1,) * (len(extent) - 1 - position))
    return gain


def scatter_about(rng, dims, width, most, cuts=(), kind=jnp.bfloat16):
    loudness = steps_of(rng, dims, cuts, -0.22, 0.18) if cuts else 1.0
    values = jax.random.normal(rng, dims, jnp.float32) * width * loudness
    return jnp.minimum(jnp.maximum(values, -most), most).astype(kind)


def setup_inputs(seed: int = 0) -> dict:
    arg_keys = jax.random.split(jax.random.key(seed), 6)
    features = scatter_about(arg_keys[0], (GRID_X, GRID_Y, CAP, VOXELS, C), 1.0, 6.0, ((0, 16), (1, 2)))
    cotangent = scatter_about(arg_keys[1], (GRID_X, GRID_Y, CAP, VOXELS, C), 1.0, 6.0, ((0, 16), (1, 2)))
    neighbours = draw_neighbours(jax.random.fold_in(arg_keys[5], 71), 0)
    weights = scatter_about(arg_keys[3], (27, C, C), (27 * C) ** -0.5, 0.109375)
    channel_gain = jnp.clip(jnp.exp(jax.random.uniform(arg_keys[4], (C,), jnp.float32, math.log(0.5), math.log(2.0))), 0.5, 2.0)
    return dict(features=features, cotangent=cotangent, neighbours=neighbours, weights=weights, channel_gain=channel_gain)


DIRECTIONS = [(a, b, c) for a in (-1, 0, 1) for b in (-1, 0, 1) for c in (-1, 0, 1)]


def rim_range(d):
    if d < 0:
        return slice(7, 8)
    if d == 0:
        return slice(0, 8)
    return slice(0, 1)


def assemble(own_blocks, gathered_table, slot_codes):
    planes = []
    for a in (-1, 0, 1):
        row_parts = []
        for b in (-1, 0, 1):
            col_parts = []
            for c in (-1, 0, 1):
                k = (a + 1) * 9 + (b + 1) * 3 + (c + 1)
                if k == 13:
                    block_piece = own_blocks
                else:
                    region = gathered_table[:, rim_range(a), rim_range(b), rim_range(c)]
                    block_piece = jnp.take(region, jnp.maximum(slot_codes[:, k], 0), axis=0)
                    present = (slot_codes[:, k] >= 0)[:, None, None, None, None]
                    block_piece = jnp.where(present, block_piece, jnp.zeros((), block_piece.dtype))
                col_parts.append(block_piece)
            row_parts.append(jnp.concatenate(col_parts, axis=3))
        planes.append(jnp.concatenate(row_parts, axis=2))
    return jnp.concatenate(planes, axis=1)


def window(padded_tile, a, b, c):
    capacity = padded_tile.shape[0]
    channels = padded_tile.shape[-1]
    return padded_tile[:, 1 + a:9 + a, 1 + b:9 + b, 1 + c:9 + c].reshape(capacity * 512, channels)


def convolve(padded_tile, weights):
    total = None
    for k in range(27):
        a, b, c = DIRECTIONS[k]
        term = jnp.dot(window(padded_tile, a, b, c), weights[k], preferred_element_type=jnp.float32)
        total = term if total is None else total + term
    return total


def convolve_adjoint(padded_tile, weights):
    total = None
    for k in range(27):
        a, b, c = DIRECTIONS[k]
        term = jnp.dot(window(padded_tile, -a, -b, -c), weights[k].T, preferred_element_type=jnp.float32)
        total = term if total is None else total + term
    return total


def weight_terms(padded_tile, scaled):
    terms = []
    for k in range(27):
        a, b, c = DIRECTIONS[k]
        terms.append(jnp.dot(window(padded_tile, a, b, c).T, scaled, preferred_element_type=jnp.float32))
    return jnp.stack(terms, axis=0)


def reference(features, cotangent, neighbours, weights, channel_gain):
    capacity = features.shape[2]
    channels = features.shape[-1]
    occupied = (neighbours[:, :, :, 13] >= 0)[..., None, None]
    masked_x = jnp.where(occupied, features, jnp.zeros((), features.dtype))
    masked_dy = jnp.where(occupied, cotangent, jnp.zeros((), cotangent.dtype))
    pad_spec = ((1, 1), (1, 1), (0, 0), (0, 0), (0, 0))
    features_pad = jnp.pad(masked_x, pad_spec)
    device_ids = jnp.arange(GRID_X * GRID_Y, dtype=jnp.int32)

    def neighbourhood(padded, device_id):
        row_index = (device_id // GRID_Y).astype(jnp.int32)
        col_index = (device_id % GRID_Y).astype(jnp.int32)
        zero_index = jnp.zeros((), jnp.int32)
        region = lax.dynamic_slice(padded, (row_index, col_index, zero_index, zero_index, zero_index),
                                   (3, 3, capacity, 512, channels))
        gathered_table = region.reshape(9 * capacity, 8, 8, 8, channels)
        own_blocks = region[1, 1].reshape(capacity, 8, 8, 8, channels)
        return gathered_table, own_blocks, row_index, col_index

    def forward_device(device_id):
        gathered_table, own_blocks, row_index, col_index = neighbourhood(features_pad, device_id)
        slot_codes = neighbours[row_index, col_index]
        tile_x = assemble(own_blocks, gathered_table, slot_codes)
        conv_out = convolve(tile_x, weights)
        pre_act = own_blocks.reshape(-1, channels).astype(jnp.float32) + channel_gain * conv_out
        sigmoid_value = jax.nn.sigmoid(pre_act)
        result = (pre_act * sigmoid_value).astype(jnp.bfloat16)
        upstream = masked_dy[row_index, col_index].reshape(-1, channels).astype(jnp.float32)
        pre_grad = upstream * sigmoid_value * (1.0 + pre_act * (1.0 - sigmoid_value))
        scaled = (channel_gain * pre_grad).astype(jnp.bfloat16)
        gain_part = jnp.sum(pre_grad * conv_out, axis=0)
        return result, pre_grad, scaled, gain_part

    results, pre_grads, scaled_all, gain_parts = lax.map(forward_device, device_ids)
    scaled_pad = jnp.pad(scaled_all.reshape(GRID_X, GRID_Y, capacity, 512, channels), pad_spec)

    def backward_device(carry, device_id):
        table_x, own_x, row_index, col_index = neighbourhood(features_pad, device_id)
        table_u, own_u, row_again, col_again = neighbourhood(scaled_pad, device_id)
        slot_codes = neighbours[row_index, col_index]
        tile_x = assemble(own_x, table_x, slot_codes)
        tile_u = assemble(own_u, table_u, slot_codes)
        grad_here = (pre_grads[device_id] + convolve_adjoint(tile_u, weights)).astype(jnp.bfloat16)
        carry = carry + weight_terms(tile_x, own_u.reshape(-1, channels))
        return carry, grad_here

    weight_grad, input_grads = lax.scan(backward_device, jnp.zeros((27, channels, channels), jnp.float32), device_ids)
    output = results.reshape(GRID_X, GRID_Y, capacity, 512, channels)
    input_grad = input_grads.reshape(GRID_X, GRID_Y, capacity, 512, channels)
    gain_grad = jnp.sum(gain_parts, axis=0)
    return (output, input_grad, weight_grad, gain_grad)
```

```python
from functools import partial

import jax
import jax.numpy as jnp
from jax import lax
from jax.experimental import pallas as pl
from jax.experimental.pallas import tpu as pltpu
from jax.sharding import PartitionSpec as P

MESH = pl.DeviceIdType.MESH
BF = jnp.bfloat16
F32 = jnp.float32
SIDES = [(a, b) for a in (-1, 0, 1) for b in (-1, 0, 1) if (a, b) != (0, 0)]
TILE = 16


class Plan:
    def __init__(self, gx, gy, rows):
        low = 4 if gx % 4 == 0 else 1
        groups = {"core": gy, "low": low, "high": gx // low}
        self.low = low
        unit = gx * gy * TILE
        units = -(-(rows + TILE) // unit)
        second = units * 2 // 7
        self.rows = units * unit
        self.streams = []
        slot = 0
        room = 0
        for start, count, order in (
            (0, units - second, ("core", "low", "high")),
            (units - second, second, ("core", "high", "low")),
        ):
            if count == 0:
                continue
            phases = []
            size = count * unit
            for name in order:
                g = groups[name]
                if g == 1:
                    continue
                size //= g
                phases.append(dict(name=name, g=g, n=size, slot=slot, room=room))
                slot += g - 1
                room += (g - 1) * size
            self.streams.append(dict(start=start * unit, rows=count * unit, phases=phases))
        self.slots = slot
        self.room = room
        self.groups = [(name, g) for name, g in groups.items() if g > 1]

    def rank(self, name, i, j):
        if name == "core":
            return j
        return lax.rem(i, self.low) if name == "low" else i // self.low

    def peer(self, name, i, j, q):
        if name == "core":
            return (i, q)
        if name == "low":
            return (i - lax.rem(i, self.low) + q, j)
        return (q * self.low + lax.rem(i, self.low), j)


def face(d):
    return slice(0, 8) if d == 0 else (slice(7, 8) if d > 0 else slice(0, 1))


def rim(d):
    return slice(0, 8) if d == 0 else (slice(7, 8) if d < 0 else slice(0, 1))


def kernel(plan, gx, gy, cap, C,
           codes, x_hbm, dy_hbm, w_hbm, gain_ref,
           out_ref, grad_ref, sum_hbm,
           gx_buf, gu_buf, even, odd, w_v, wt_v, dy_v, pg_v, s_v, acc, send, recv, whole,
           in_sem, xs_sem, xr_sem, us_sem, ur_sem, rs_s, rs_r, ag_s, ag_r):
    i = lax.axis_index("gx")
    j = lax.axis_index("gy")
    V = 512

    def inside(a, b):
        ok = None
        for t in ([i + a >= 0] if a < 0 else []) + ([i + a < gx] if a > 0 else []) + (
                [j + b >= 0] if b < 0 else []) + ([j + b < gy] if b > 0 else []):
            ok = t if ok is None else jnp.logical_and(ok, t)
        return ok

    own = pl.ds(4 * cap, cap)
    load_x = pltpu.make_async_copy(x_hbm, gx_buf.at[own], in_sem.at[0])
    load_w = pltpu.make_async_copy(w_hbm, w_v, in_sem.at[1])
    load_dy = pltpu.make_async_copy(dy_hbm, dy_v, in_sem.at[2])
    load_x.start()
    load_w.start()
    load_dy.start()

    barrier = pltpu.get_barrier_semaphore()
    count = jnp.int32(sum(g - 1 for _, g in plan.groups))
    for a, b in SIDES:
        ok = inside(a, b)
        count = count + ok.astype(jnp.int32)

        @pl.when(ok)
        def _():
            pl.semaphore_signal(barrier, inc=1, device_id=(i + a, j + b), device_id_type=MESH)

    for name, g in plan.groups:
        r = plan.rank(name, i, j)
        for d in range(1, g):
            pl.semaphore_signal(barrier, inc=1, device_id=plan.peer(name, i, j, lax.rem(r + d, g)),
                                device_id_type=MESH)
    pl.semaphore_wait(barrier, count)

    def halo(src, buf, ssem, rsem, m):
        a, b = SIDES[m]
        back = pl.ds((3 * (1 - a) + (1 - b)) * cap, cap)
        return pltpu.make_async_remote_copy(
            src_ref=src.at[:, face(a), face(b)], dst_ref=buf.at[back, face(a), face(b)],
            send_sem=ssem.at[m], recv_sem=rsem.at[m], device_id=(i + a, j + b), device_id_type=MESH)

    def halo_start(src, buf, ssem, rsem):
        for m, (a, b) in enumerate(SIDES):
            @pl.when(inside(a, b))
            def _():
                halo(src, buf, ssem, rsem, m).start()

    def halo_wait(src, buf, ssem, rsem):
        for m, (a, b) in enumerate(SIDES):
            @pl.when(inside(-a, -b))
            def _():
                halo(src, buf, ssem, rsem, m).wait_recv()

            @pl.when(inside(a, b))
            def _():
                halo(src, buf, ssem, rsem, m).wait_send()

    halo_start(x_hbm, gx_buf, xs_sem, xr_sem)

    load_w.wait()
    for k in range(27):
        wt_v[k] = w_v[26 - k].astype(F32).T.astype(BF)
    load_x.wait()
    load_dy.wait()
    halo_wait(x_hbm, gx_buf, xs_sem, xr_sem)

    def piece(buf, s, x, a, b, c):
        k = 9 * (a + 1) + 3 * (b + 1) + (c + 1)
        code = codes[s, k]
        if k == 13:
            value = buf[4 * cap + s, x]
        else:
            value = buf[jnp.maximum(code, 0), x, rim(b)]
        value = value.astype(F32)
        return jnp.where(jnp.full(value.shape, code, jnp.int32) >= 0, value, 0.0)

    def plane(buf, s, px, x, a):
        level = [jnp.concatenate([piece(buf, s, x, a, b, c) for b in (-1, 0, 1)], axis=0) for c in (-1, 0, 1)]
        z = lax.broadcasted_iota(jnp.int32, level[1].shape, 1)
        down = pltpu.roll(jnp.where(z == 7, level[0], level[1]), 1, 1)
        up = pltpu.roll(jnp.where(z == 0, level[2], level[1]), 7, 1)
        for c, value in enumerate((down, level[1], up)):
            lanes = slice(c * C, (c + 1) * C)
            even[s, px, :, :, lanes] = value.reshape(80, C).astype(BF).reshape(5, 16, C)
            odd[s, px, :, :, lanes] = value[1:9].reshape(64, C).astype(BF).reshape(4, 16, C)

    def build(buf):
        for s in range(cap):
            plane(buf, s, 0, 7, -1)

            @pl.loop(0, 8)
            def _(x):
                plane(buf, s, x + 1, x, 0)

            plane(buf, s, 9, 0, 1)

    def window(s, a, b):
        xs = slice(1 + a, 9 + a)
        if b == 0:
            return odd[s, xs].reshape(V, 3 * C)
        return (even[s, xs, 0:4] if b < 0 else even[s, xs, 1:5]).reshape(V, 3 * C)

    def conv(s, w):
        total = None
        for m in range(9):
            term = jnp.dot(window(s, m // 3 - 1, m % 3 - 1), w[3 * m:3 * m + 3].reshape(3 * C, C),
                           preferred_element_type=F32)
            total = term if total is None else total + term
        return total

    build(gx_buf)
    gain = gain_ref[...]
    gain_sum = jnp.zeros((1, C), F32)
    for s in range(cap):
        c_out = conv(s, w_v)
        full = jnp.full((V, C), codes[s, 13], jnp.int32) >= 0
        mx = jnp.where(full, gx_buf[4 * cap + s].astype(F32).reshape(V, C), 0.0)
        pre = mx + gain * c_out
        sig = jax.nn.sigmoid(pre)
        out_ref[s] = (pre * sig).astype(BF)
        dy = jnp.where(full, dy_v[s].astype(F32), 0.0)
        pg = dy * sig * (1.0 + pre * (1.0 - sig))
        pg_v[s] = pg
        scaled = gain * pg
        gu_buf[4 * cap + s] = scaled.reshape(8, 8, 8, C).astype(BF)
        s_v[:, s * V:(s + 1) * V] = scaled.T.astype(BF)
        gain_sum = gain_sum + jnp.sum(pg * c_out, axis=0, keepdims=True)

    u_src = gu_buf.at[own]
    halo_start(u_src, gu_buf, us_sem, ur_sem)

    for m in range(9):
        total = None
        for s in range(cap):
            term = jnp.dot(s_v[:, s * V:(s + 1) * V], window(s, m // 3 - 1, m % 3 - 1), preferred_element_type=F32)
            total = term if total is None else total + term
        rows = slice(m * 3 * C, (m + 1) * 3 * C)
        value = total.T
        acc[rows] = value
        send[rows] = value.astype(BF)
    last = 27 * C
    value = jnp.broadcast_to(gain_sum, (TILE, C))
    acc[last:last + TILE] = value
    send[last:last + TILE] = value.astype(BF)
    rest = plan.rows - last - TILE
    if rest:
        acc[last + TILE:] = jnp.zeros((rest, C), F32)
        send[last + TILE:] = jnp.zeros((rest, C), BF)

    base = [[jnp.int32(st["start"])] for st in plan.streams]

    def rows_at(offset, n):
        return pl.ds(pl.multiple_of(offset, TILE), n)

    def scatter(t, p):
        ph = plan.streams[t]["phases"][p]
        r = plan.rank(ph["name"], i, j)
        copies = []
        for d in range(1, ph["g"]):
            q = lax.rem(r + d, ph["g"])
            copies.append(pltpu.make_async_remote_copy(
                src_ref=send.at[rows_at(base[t][p] + q * ph["n"], ph["n"])],
                dst_ref=recv.at[pl.ds(ph["room"] + (d - 1) * ph["n"], ph["n"])],
                send_sem=rs_s.at[ph["slot"] + d - 1], recv_sem=rs_r.at[ph["slot"] + d - 1],
                device_id=plan.peer(ph["name"], i, j, q), device_id_type=MESH))
        for c in copies:
            c.start()
        return copies

    def gather(t, p):
        ph = plan.streams[t]["phases"][p]
        r = plan.rank(ph["name"], i, j)
        mine = rows_at(base[t][p] + r * ph["n"], ph["n"])
        copies = []
        for d in range(1, ph["g"]):
            q = lax.rem(r + d, ph["g"])
            copies.append(pltpu.make_async_remote_copy(
                src_ref=whole.at[mine], dst_ref=whole.at[mine],
                send_sem=ag_s.at[ph["slot"] + d - 1], recv_sem=ag_r.at[ph["slot"] + d - 1],
                device_id=plan.peer(ph["name"], i, j, q), device_id_type=MESH))
        for c in copies:
            c.start()
        return copies

    def reduce(t, p, copies):
        phases = plan.streams[t]["phases"]
        ph = phases[p]
        r = plan.rank(ph["name"], i, j)
        for c in copies:
            c.wait()
        here = base[t][p] + r * ph["n"]
        base[t].append(here)
        mine = rows_at(here, ph["n"])
        value = acc[mine]
        for d in range(1, ph["g"]):
            value = value + recv[pl.ds(ph["room"] + (d - 1) * ph["n"], ph["n"])].astype(F32)
        if p + 1 < len(phases):
            acc[mine] = value
            send[mine] = value.astype(BF)
        else:
            whole[mine] = value.astype(BF)

    def advance(pending, p):
        for t, st in enumerate(plan.streams):
            steps = len(st["phases"])
            if p < steps:
                reduce(t, p, pending[t])
            else:
                for c in pending[t] or ():
                    c.wait()
            if p + 1 < steps:
                pending[t] = scatter(t, p + 1)
            elif 2 * steps - p - 2 >= 0:
                pending[t] = gather(t, 2 * steps - p - 2)
            else:
                pending[t] = None

    pending = [scatter(t, 0) for t in range(len(plan.streams))]
    halo_wait(u_src, gu_buf, us_sem, ur_sem)
    build(gu_buf)
    advance(pending, 0)
    for s in range(cap):
        grad_ref[s] = (pg_v[s] + conv(s, wt_v)).astype(BF)
        if s == 0:
            advance(pending, 1)
    steps = max(len(st["phases"]) for st in plan.streams)
    for p in range(2, 2 * steps):
        advance(pending, p)
    done = pltpu.make_async_copy(whole, sum_hbm, in_sem.at[3])
    done.start()
    done.wait()


def on_device(gx, gy, features, cotangent, neighbours, weights, channel_gain):
    cap, C = features.shape[2], features.shape[-1]
    plan = Plan(gx, gy, 27 * C)
    V = 512
    hbm = pl.BlockSpec(memory_space=pl.ANY)
    vmem = pl.BlockSpec(memory_space=pltpu.VMEM)
    dma = pltpu.SemaphoreType.DMA
    out, grad, total = pl.pallas_call(
        partial(kernel, plan, gx, gy, cap, C),
        out_shape=(
            jax.ShapeDtypeStruct((cap, V, C), BF),
            jax.ShapeDtypeStruct((cap, V, C), BF),
            jax.ShapeDtypeStruct((plan.rows, C), BF),
        ),
        in_specs=[pl.BlockSpec(memory_space=pltpu.SMEM), hbm, hbm, hbm, vmem],
        out_specs=(vmem, vmem, hbm),
        scratch_shapes=[
            pltpu.VMEM((9 * cap, 8, 8, 8, C), BF),
            pltpu.VMEM((9 * cap, 8, 8, 8, C), BF),
            pltpu.VMEM((cap, 10, 5, 16, 3 * C), BF),
            pltpu.VMEM((cap, 10, 4, 16, 3 * C), BF),
            pltpu.VMEM((27, C, C), BF),
            pltpu.VMEM((27, C, C), BF),
            pltpu.VMEM((cap, V, C), BF),
            pltpu.VMEM((cap, V, C), F32),
            pltpu.VMEM((C, cap * V), BF),
            pltpu.VMEM((plan.rows, C), F32),
            pltpu.VMEM((plan.rows, C), BF),
            pltpu.VMEM((plan.room, C), BF),
            pltpu.VMEM((plan.rows, C), BF),
            dma((4,)), dma((8,)), dma((8,)), dma((8,)), dma((8,)),
            dma((plan.slots,)), dma((plan.slots,)), dma((plan.slots,)), dma((plan.slots,)),
        ],
        compiler_params=pltpu.CompilerParams(
            collective_id=0, has_side_effects=True, vmem_limit_bytes=60 * 1024 * 1024),
    )(
        neighbours.reshape(cap, 27),
        features.reshape(cap, 8, 8, 8, C),
        cotangent.reshape(cap, V, C),
        weights,
        channel_gain.reshape(1, C),
    )
    shape = (1, 1, cap, V, C)
    weight_grad = total[: 27 * C].astype(F32).reshape(27, C, C)
    gain_grad = total[27 * C].astype(F32)
    return out.reshape(shape), grad.reshape(shape), weight_grad, gain_grad


def solution(mesh):
    spec = P("gx", "gy", None, None, None)
    return jax.shard_map(
        partial(on_device, mesh.shape["gx"], mesh.shape["gy"]),
        mesh=mesh,
        in_specs=(spec, spec, P("gx", "gy", None, None), P(), P()),
        out_specs=(spec, spec, P(), P()),
        check_vma=False,
    )
```

```python
from functools import partial

import jax
import jax.numpy as jnp
from jax import lax
from jax.experimental import pallas as pl
from jax.experimental.pallas import tpu as pltpu
from jax.sharding import PartitionSpec as P

MESH = pl.DeviceIdType.MESH
BF = jnp.bfloat16
F32 = jnp.float32
SIDES = [(a, b) for a in (-1, 0, 1) for b in (-1, 0, 1) if (a, b) != (0, 0)]
TILE = 16


class Plan:
    def __init__(self, gx, gy, rows):
        low = 4 if gx % 4 == 0 else 1
        groups = {"core": gy, "low": low, "high": gx // low}
        self.low = low
        unit = gx * gy * TILE
        units = -(-rows // unit)
        second = units * 2 // 7
        self.rows = units * unit
        self.streams = []
        slot = 0
        room = 0
        for start, count, order in (
            (0, units - second, ("core", "low", "high")),
            (units - second, second, ("core", "high", "low")),
        ):
            if count == 0:
                continue
            phases = []
            size = count * unit
            for name in order:
                g = groups[name]
                if g == 1:
                    continue
                size //= g
                phases.append(dict(name=name, g=g, n=size, slot=slot, room=room))
                slot += g - 1
                room += (g - 1) * size
            self.streams.append(dict(start=start * unit, rows=count * unit, phases=phases))
        self.slots = slot
        self.room = room
        self.groups = [(name, g) for name, g in groups.items() if g > 1]
        self.members = sum(g for _, g in self.groups)

    def rank(self, name, i, j):
        if name == "core":
            return j
        return lax.rem(i, self.low) if name == "low" else i // self.low

    def peer(self, name, i, j, q):
        if name == "core":
            return (i, q)
        if name == "low":
            return (i - lax.rem(i, self.low) + q, j)
        return (q * self.low + lax.rem(i, self.low), j)


def face(d):
    return slice(0, 8) if d == 0 else (slice(7, 8) if d > 0 else slice(0, 1))


def rim(d):
    return slice(0, 8) if d == 0 else (slice(7, 8) if d < 0 else slice(0, 1))


def kernel(plan, gx, gy, cap, C,
           codes, x_hbm, dy_hbm, w_hbm, gain_ref,
           out_ref, grad_ref, sum_ref, gsum_ref,
           gx_buf, gu_buf, even, odd, w_v, wt_v, dy_v, pg_v, s_v, acc, send, recv, whole, gbuf,
           in_sem, xs_sem, xr_sem, us_sem, ur_sem, rs_s, rs_r, ag_s, ag_r, g_s, g_r):
    i = lax.axis_index("gx")
    j = lax.axis_index("gy")
    V = 512

    def inside(a, b):
        ok = None
        for t in ([i + a >= 0] if a < 0 else []) + ([i + a < gx] if a > 0 else []) + (
                [j + b >= 0] if b < 0 else []) + ([j + b < gy] if b > 0 else []):
            ok = t if ok is None else jnp.logical_and(ok, t)
        return ok

    own = pl.ds(4 * cap, cap)
    load_x = pltpu.make_async_copy(x_hbm, gx_buf.at[own], in_sem.at[0])
    load_w = pltpu.make_async_copy(w_hbm, w_v, in_sem.at[1])
    load_dy = pltpu.make_async_copy(dy_hbm, dy_v, in_sem.at[2])
    load_x.start()
    load_w.start()
    load_dy.start()

    barrier = pltpu.get_barrier_semaphore()
    count = jnp.int32(sum(g - 1 for _, g in plan.groups))
    for a, b in SIDES:
        ok = inside(a, b)
        count = count + ok.astype(jnp.int32)

        @pl.when(ok)
        def _():
            pl.semaphore_signal(barrier, inc=1, device_id=(i + a, j + b), device_id_type=MESH)

    for name, g in plan.groups:
        r = plan.rank(name, i, j)
        for d in range(1, g):
            pl.semaphore_signal(barrier, inc=1, device_id=plan.peer(name, i, j, lax.rem(r + d, g)),
                                device_id_type=MESH)
    pl.semaphore_wait(barrier, count)

    def halo(src, buf, ssem, rsem, m):
        a, b = SIDES[m]
        back = pl.ds((3 * (1 - a) + (1 - b)) * cap, cap)
        return pltpu.make_async_remote_copy(
            src_ref=src.at[:, face(a), face(b)], dst_ref=buf.at[back, face(a), face(b)],
            send_sem=ssem.at[m], recv_sem=rsem.at[m], device_id=(i + a, j + b), device_id_type=MESH)

    def halo_start(src, buf, ssem, rsem):
        for m, (a, b) in enumerate(SIDES):
            @pl.when(inside(a, b))
            def _():
                halo(src, buf, ssem, rsem, m).start()

    def halo_wait(src, buf, ssem, rsem):
        for m, (a, b) in enumerate(SIDES):
            @pl.when(inside(-a, -b))
            def _():
                halo(src, buf, ssem, rsem, m).wait_recv()

            @pl.when(inside(a, b))
            def _():
                halo(src, buf, ssem, rsem, m).wait_send()

    halo_start(x_hbm, gx_buf, xs_sem, xr_sem)

    load_w.wait()
    for k in range(27):
        wt_v[k] = w_v[26 - k].astype(F32).T.astype(BF)
    load_x.wait()
    load_dy.wait()
    halo_wait(x_hbm, gx_buf, xs_sem, xr_sem)

    def piece(buf, s, x, a, b, c):
        k = 9 * (a + 1) + 3 * (b + 1) + (c + 1)
        code = codes[s, k]
        if k == 13:
            value = buf[4 * cap + s, x]
        else:
            value = buf[jnp.maximum(code, 0), x, rim(b)]
        value = value.astype(F32)
        return jnp.where(jnp.full(value.shape, code, jnp.int32) >= 0, value, 0.0)

    def plane(buf, s, px, x, a):
        level = [jnp.concatenate([piece(buf, s, x, a, b, c) for b in (-1, 0, 1)], axis=0) for c in (-1, 0, 1)]
        z = lax.broadcasted_iota(jnp.int32, level[1].shape, 1)
        down = pltpu.roll(jnp.where(z == 7, level[0], level[1]), 1, 1)
        up = pltpu.roll(jnp.where(z == 0, level[2], level[1]), 7, 1)
        for c, value in enumerate((down, level[1], up)):
            lanes = slice(c * C, (c + 1) * C)
            even[s, px, :, :, lanes] = value.reshape(80, C).astype(BF).reshape(5, 16, C)
            odd[s, px, :, :, lanes] = value[1:9].reshape(64, C).astype(BF).reshape(4, 16, C)

    def build(buf):
        for s in range(cap):
            plane(buf, s, 0, 7, -1)

            @pl.loop(0, 8)
            def _(x):
                plane(buf, s, x + 1, x, 0)

            plane(buf, s, 9, 0, 1)

    def window(s, a, b):
        xs = slice(1 + a, 9 + a)
        if b == 0:
            return odd[s, xs].reshape(V, 3 * C)
        return (even[s, xs, 0:4] if b < 0 else even[s, xs, 1:5]).reshape(V, 3 * C)

    def conv(s, w):
        total = None
        for m in range(9):
            term = jnp.dot(window(s, m // 3 - 1, m % 3 - 1), w[3 * m:3 * m + 3].reshape(3 * C, C),
                           preferred_element_type=F32)
            total = term if total is None else total + term
        return total

    build(gx_buf)
    gain = gain_ref[...]
    gain_sum = jnp.zeros((1, C), F32)
    for s in range(cap):
        c_out = conv(s, w_v)
        full = jnp.full((V, C), codes[s, 13], jnp.int32) >= 0
        mx = jnp.where(full, gx_buf[4 * cap + s].astype(F32).reshape(V, C), 0.0)
        pre = mx + gain * c_out
        sig = jax.nn.sigmoid(pre)
        out_ref[s] = (pre * sig).astype(BF)
        dy = jnp.where(full, dy_v[s].astype(F32), 0.0)
        pg = dy * sig * (1.0 + pre * (1.0 - sig))
        pg_v[s] = pg
        scaled = gain * pg
        gu_buf[4 * cap + s] = scaled.reshape(8, 8, 8, C).astype(BF)
        s_v[:, s * V:(s + 1) * V] = scaled.T.astype(BF)
        gain_sum = gain_sum + jnp.sum(pg * c_out, axis=0, keepdims=True)

    u_src = gu_buf.at[own]
    halo_start(u_src, gu_buf, us_sem, ur_sem)

    for m in range(9):
        total = None
        for s in range(cap):
            term = jnp.dot(s_v[:, s * V:(s + 1) * V], window(s, m // 3 - 1, m % 3 - 1), preferred_element_type=F32)
            total = term if total is None else total + term
        rows = slice(m * 3 * C, (m + 1) * 3 * C)
        value = total.T
        acc[rows] = value
        send[rows] = value.astype(BF)
    last = 27 * C
    rest = plan.rows - last
    if rest:
        acc[last:] = jnp.zeros((rest, C), F32)
        send[last:] = jnp.zeros((rest, C), BF)

    base = [[jnp.int32(st["start"])] for st in plan.streams]

    def rows_at(offset, n):
        return pl.ds(pl.multiple_of(offset, TILE), n)

    def scatter(t, p):
        ph = plan.streams[t]["phases"][p]
        r = plan.rank(ph["name"], i, j)
        copies = []
        for d in range(1, ph["g"]):
            q = lax.rem(r + d, ph["g"])
            copies.append(pltpu.make_async_remote_copy(
                src_ref=send.at[rows_at(base[t][p] + q * ph["n"], ph["n"])],
                dst_ref=recv.at[pl.ds(ph["room"] + (d - 1) * ph["n"], ph["n"])],
                send_sem=rs_s.at[ph["slot"] + d - 1], recv_sem=rs_r.at[ph["slot"] + d - 1],
                device_id=plan.peer(ph["name"], i, j, q), device_id_type=MESH))
        for c in copies:
            c.start()
        return copies

    def gather(t, p):
        ph = plan.streams[t]["phases"][p]
        r = plan.rank(ph["name"], i, j)
        mine = rows_at(base[t][p] + r * ph["n"], ph["n"])
        copies = []
        for d in range(1, ph["g"]):
            q = lax.rem(r + d, ph["g"])
            copies.append(pltpu.make_async_remote_copy(
                src_ref=whole.at[mine], dst_ref=whole.at[mine],
                send_sem=ag_s.at[ph["slot"] + d - 1], recv_sem=ag_r.at[ph["slot"] + d - 1],
                device_id=plan.peer(ph["name"], i, j, q), device_id_type=MESH))
        for c in copies:
            c.start()
        return copies

    def reduce(t, p, copies):
        phases = plan.streams[t]["phases"]
        ph = phases[p]
        r = plan.rank(ph["name"], i, j)
        for c in copies:
            c.wait()
        here = base[t][p] + r * ph["n"]
        base[t].append(here)
        mine = rows_at(here, ph["n"])
        value = acc[mine]
        for d in range(1, ph["g"]):
            value = value + recv[pl.ds(ph["room"] + (d - 1) * ph["n"], ph["n"])].astype(F32)
        if p + 1 < len(phases):
            acc[mine] = value
            send[mine] = value.astype(BF)
        else:
            whole[mine] = value.astype(BF)

    def advance(pending, p):
        for t, st in enumerate(plan.streams):
            steps = len(st["phases"])
            if p < steps:
                reduce(t, p, pending[t])
            else:
                for c in pending[t] or ():
                    c.wait()
            if p + 1 < steps:
                pending[t] = scatter(t, p + 1)
            elif 2 * steps - p - 2 >= 0:
                pending[t] = gather(t, 2 * steps - p - 2)
            else:
                pending[t] = None

    starts = [sum(g for _, g in plan.groups[:h]) for h in range(len(plan.groups))]

    def gain_send(h, value):
        name, g = plan.groups[h]
        r = plan.rank(name, i, j)
        gbuf[starts[h] + r] = jnp.broadcast_to(value, (8, C))
        copies = []
        for d in range(1, g):
            copies.append(pltpu.make_async_remote_copy(
                src_ref=gbuf.at[starts[h] + r], dst_ref=gbuf.at[starts[h] + r],
                send_sem=g_s.at[starts[h] + d], recv_sem=g_r.at[starts[h] + d],
                device_id=plan.peer(name, i, j, lax.rem(r + d, g)), device_id_type=MESH))
        for c in copies:
            c.start()
        return copies

    def gain_sum_of(h, copies):
        for c in copies:
            c.wait()
        value = gbuf[starts[h]]
        for q in range(1, plan.groups[h][1]):
            value = value + gbuf[starts[h] + q]
        return value

    pending = [scatter(t, 0) for t in range(len(plan.streams))]
    value = gain_sum
    flight = gain_send(0, value) if plan.groups else None
    advance(pending, 0)
    for h in range(1, len(plan.groups)):
        if h == 1:
            value = gain_sum_of(0, flight)
            flight = gain_send(1, value)
    halo_wait(u_src, gu_buf, us_sem, ur_sem)
    build(gu_buf)
    for s in range(cap):
        grad_ref[s] = (pg_v[s] + conv(s, wt_v)).astype(BF)
    steps = max(len(st["phases"]) for st in plan.streams)
    for p in range(1, 2 * steps):
        advance(pending, p)
        if p < len(plan.groups):
            value = gain_sum_of(p, flight)
            if p + 1 < len(plan.groups):
                flight = gain_send(p + 1, value)
    gsum_ref[...] = value
    sum_ref[...] = whole[0:27 * C]


def finish(out_ref, grad_ref, sum_ref, gsum_ref, out_hbm, grad_hbm, sum_hbm, gsum_out, wide, sems):
    copies = [pltpu.make_async_copy(out_ref, out_hbm, sems.at[0]),
              pltpu.make_async_copy(grad_ref, grad_hbm, sems.at[1])]
    for c in copies:
        c.start()
    n = wide.shape[0] // 9
    for m in range(9):
        rows = pl.ds(m * n, n)
        wide[rows] = sum_ref[rows].astype(F32)
        copies.append(pltpu.make_async_copy(wide.at[rows], sum_hbm.at[rows], sems.at[2 + m]))
        copies[-1].start()
    gsum_out[...] = gsum_ref[0:1]
    for c in copies:
        c.wait()


def on_device(gx, gy, features, cotangent, neighbours, weights, channel_gain):
    cap, C = features.shape[2], features.shape[-1]
    plan = Plan(gx, gy, 27 * C)
    V = 512
    hbm = pl.BlockSpec(memory_space=pl.ANY)
    far = pl.BlockSpec(memory_space=pltpu.HBM)
    vmem = pl.BlockSpec(memory_space=pltpu.VMEM)
    dma = pltpu.SemaphoreType.DMA
    parts = pl.pallas_call(
        partial(kernel, plan, gx, gy, cap, C),
        out_shape=(
            pltpu.VMEM((cap, V, C), BF),
            pltpu.VMEM((cap, V, C), BF),
            pltpu.VMEM((27 * C, C), BF),
            pltpu.VMEM((8, C), F32),
        ),
        in_specs=[pl.BlockSpec(memory_space=pltpu.SMEM), far, far, far, vmem],
        out_specs=(vmem, vmem, vmem, vmem),
        scratch_shapes=[
            pltpu.VMEM((9 * cap, 8, 8, 8, C), BF),
            pltpu.VMEM((9 * cap, 8, 8, 8, C), BF),
            pltpu.VMEM((cap, 10, 5, 16, 3 * C), BF),
            pltpu.VMEM((cap, 10, 4, 16, 3 * C), BF),
            pltpu.VMEM((27, C, C), BF),
            pltpu.VMEM((27, C, C), BF),
            pltpu.VMEM((cap, V, C), BF),
            pltpu.VMEM((cap, V, C), F32),
            pltpu.VMEM((C, cap * V), BF),
            pltpu.VMEM((plan.rows, C), F32),
            pltpu.VMEM((plan.rows, C), BF),
            pltpu.VMEM((plan.room, C), BF),
            pltpu.VMEM((plan.rows, C), BF),
            pltpu.VMEM((plan.members, 8, C), F32),
            dma((3,)), dma((8,)), dma((8,)), dma((8,)), dma((8,)),
            dma((plan.slots,)), dma((plan.slots,)), dma((plan.slots,)), dma((plan.slots,)),
            dma((plan.members,)), dma((plan.members,)),
        ],
        compiler_params=pltpu.CompilerParams(
            collective_id=0, has_side_effects=True, vmem_limit_bytes=62 * 1024 * 1024),
    )(
        neighbours.reshape(cap, 27),
        features.reshape(cap, 8, 8, 8, C),
        cotangent.reshape(cap, V, C),
        weights,
        channel_gain.reshape(1, C),
    )
    shape = (1, 1, cap, V, C)
    out, grad, weight_grad, gain_grad = pl.pallas_call(
        finish,
        out_shape=(
            jax.ShapeDtypeStruct((cap, V, C), BF),
            jax.ShapeDtypeStruct((cap, V, C), BF),
            jax.ShapeDtypeStruct((27 * C, C), F32),
            jax.ShapeDtypeStruct((1, C), F32),
        ),
        in_specs=[vmem] * 4,
        out_specs=(hbm, hbm, hbm, vmem),
        scratch_shapes=[pltpu.VMEM((27 * C, C), F32), dma((11,))],
        compiler_params=pltpu.CompilerParams(vmem_limit_bytes=16 * 1024 * 1024),
    )(*parts)
    return out.reshape(shape), grad.reshape(shape), weight_grad.reshape(27, C, C), gain_grad.reshape(C)


def solution(mesh):
    spec = P("gx", "gy", None, None, None)
    return jax.shard_map(
        partial(on_device, mesh.shape["gx"], mesh.shape["gy"]),
        mesh=mesh,
        in_specs=(spec, spec, P("gx", "gy", None, None), P(), P()),
        out_specs=(spec, spec, P(), P()),
        check_vma=False,
    )
```

```python
from functools import partial

import jax
import jax.numpy as jnp
from jax import lax
from jax.experimental import pallas as pl
from jax.experimental.pallas import tpu as pltpu
from jax.sharding import PartitionSpec as P

MESH = pl.DeviceIdType.MESH
BF = jnp.bfloat16
F32 = jnp.float32
ORDERS = (("core", "low", "high"), ("core", "low", "high"), ("core", "high", "low"))
CUTS = (0, 3, 5, 7)
SIDES = [(a, b) for a in (-1, 0, 1) for b in (-1, 0, 1) if (a, b) != (0, 0)]
TILE = 16


class Plan:
    def __init__(self, gx, gy, rows):
        low = 4 if gx % 4 == 0 else 1
        groups = {"core": gy, "low": low, "high": gx // low}
        self.low = low
        unit = gx * gy * TILE
        units = -(-rows // unit)
        cuts = [units * part // 7 for part in CUTS]
        self.rows = units * unit
        self.streams = []
        slot = 0
        room = 0
        for start, stop, order in zip(cuts[:-1], cuts[1:], ORDERS):
            count = stop - start
            if count == 0:
                continue
            phases = []
            size = count * unit
            for name in order:
                g = groups[name]
                if g == 1:
                    continue
                size //= g
                phases.append(dict(name=name, g=g, n=size, slot=slot, room=room))
                slot += g - 1
                room += (g - 1) * size
            self.streams.append(dict(start=start * unit, rows=count * unit, phases=phases))
        self.slots = slot
        self.room = room
        self.groups = [(name, g) for name, g in groups.items() if g > 1]
        self.members = sum(g for _, g in self.groups)

    def rank(self, name, i, j):
        if name == "core":
            return j
        return lax.rem(i, self.low) if name == "low" else i // self.low

    def peer(self, name, i, j, q):
        if name == "core":
            return (i, q)
        if name == "low":
            return (i - lax.rem(i, self.low) + q, j)
        return (q * self.low + lax.rem(i, self.low), j)


def face(d):
    return slice(0, 8) if d == 0 else (slice(7, 8) if d > 0 else slice(0, 1))


def rim(d):
    return slice(0, 8) if d == 0 else (slice(7, 8) if d < 0 else slice(0, 1))


def kernel(plan, gx, gy, cap, C,
           codes, x_hbm, dy_hbm, w_hbm, gain_ref,
           out_ref, grad_ref, sum_ref, gsum_ref,
           gx_buf, gu_buf, even, odd, w_v, wt_v, dy_v, pg_v, s_v, acc, send, recv, whole, gbuf,
           in_sem, xs_sem, xr_sem, us_sem, ur_sem, rs_s, rs_r, ag_s, ag_r, g_s, g_r):
    i = lax.axis_index("gx")
    j = lax.axis_index("gy")
    V = 512

    def inside(a, b):
        ok = None
        for t in ([i + a >= 0] if a < 0 else []) + ([i + a < gx] if a > 0 else []) + (
                [j + b >= 0] if b < 0 else []) + ([j + b < gy] if b > 0 else []):
            ok = t if ok is None else jnp.logical_and(ok, t)
        return ok

    own = pl.ds(4 * cap, cap)
    load_x = pltpu.make_async_copy(x_hbm, gx_buf.at[own], in_sem.at[0])
    load_w = pltpu.make_async_copy(w_hbm, w_v, in_sem.at[1])
    load_dy = pltpu.make_async_copy(dy_hbm, dy_v, in_sem.at[2])
    load_x.start()
    load_w.start()
    load_dy.start()

    barrier = pltpu.get_barrier_semaphore()
    count = jnp.int32(sum(g - 1 for _, g in plan.groups))
    for a, b in SIDES:
        ok = inside(a, b)
        count = count + ok.astype(jnp.int32)

        @pl.when(ok)
        def _():
            pl.semaphore_signal(barrier, inc=1, device_id=(i + a, j + b), device_id_type=MESH)

    for name, g in plan.groups:
        r = plan.rank(name, i, j)
        for d in range(1, g):
            pl.semaphore_signal(barrier, inc=1, device_id=plan.peer(name, i, j, lax.rem(r + d, g)),
                                device_id_type=MESH)
    pl.semaphore_wait(barrier, count)

    def halo(src, buf, ssem, rsem, m):
        a, b = SIDES[m]
        back = pl.ds((3 * (1 - a) + (1 - b)) * cap, cap)
        return pltpu.make_async_remote_copy(
            src_ref=src.at[:, face(a), face(b)], dst_ref=buf.at[back, face(a), face(b)],
            send_sem=ssem.at[m], recv_sem=rsem.at[m], device_id=(i + a, j + b), device_id_type=MESH)

    def halo_start(src, buf, ssem, rsem):
        for m, (a, b) in enumerate(SIDES):
            @pl.when(inside(a, b))
            def _():
                halo(src, buf, ssem, rsem, m).start()

    def halo_wait(src, buf, ssem, rsem):
        for m, (a, b) in enumerate(SIDES):
            @pl.when(inside(-a, -b))
            def _():
                halo(src, buf, ssem, rsem, m).wait_recv()

            @pl.when(inside(a, b))
            def _():
                halo(src, buf, ssem, rsem, m).wait_send()

    halo_start(x_hbm, gx_buf, xs_sem, xr_sem)

    load_w.wait()
    for k in range(27):
        wt_v[k] = w_v[26 - k].astype(F32).T.astype(BF)
    load_x.wait()
    load_dy.wait()
    halo_wait(x_hbm, gx_buf, xs_sem, xr_sem)

    def piece(buf, s, x, a, b, c):
        k = 9 * (a + 1) + 3 * (b + 1) + (c + 1)
        code = codes[s, k]
        if k == 13:
            value = buf[4 * cap + s, x]
        else:
            value = buf[jnp.maximum(code, 0), x, rim(b)]
        value = value.astype(F32)
        return jnp.where(jnp.full(value.shape, code, jnp.int32) >= 0, value, 0.0)

    def plane(buf, s, px, x, a):
        level = [jnp.concatenate([piece(buf, s, x, a, b, c) for b in (-1, 0, 1)], axis=0) for c in (-1, 0, 1)]
        z = lax.broadcasted_iota(jnp.int32, level[1].shape, 1)
        down = pltpu.roll(jnp.where(z == 7, level[0], level[1]), 1, 1)
        up = pltpu.roll(jnp.where(z == 0, level[2], level[1]), 7, 1)
        for c, value in enumerate((down, level[1], up)):
            lanes = slice(c * C, (c + 1) * C)
            even[s, px, :, :, lanes] = value.reshape(80, C).astype(BF).reshape(5, 16, C)
            odd[s, px, :, :, lanes] = value[1:9].reshape(64, C).astype(BF).reshape(4, 16, C)

    def build(buf):
        for s in range(cap):
            plane(buf, s, 0, 7, -1)

            @pl.loop(0, 8)
            def _(x):
                plane(buf, s, x + 1, x, 0)

            plane(buf, s, 9, 0, 1)

    def window(s, a, b):
        xs = slice(1 + a, 9 + a)
        if b == 0:
            return odd[s, xs].reshape(V, 3 * C)
        return (even[s, xs, 0:4] if b < 0 else even[s, xs, 1:5]).reshape(V, 3 * C)

    def conv(s, w):
        total = None
        for m in range(9):
            term = jnp.dot(window(s, m // 3 - 1, m % 3 - 1), w[3 * m:3 * m + 3].reshape(3 * C, C),
                           preferred_element_type=F32)
            total = term if total is None else total + term
        return total

    build(gx_buf)
    gain = gain_ref[...]
    gain_sum = jnp.zeros((1, C), F32)
    for s in range(cap):
        c_out = conv(s, w_v)
        full = jnp.full((V, C), codes[s, 13], jnp.int32) >= 0
        mx = jnp.where(full, gx_buf[4 * cap + s].astype(F32).reshape(V, C), 0.0)
        pre = mx + gain * c_out
        sig = jax.nn.sigmoid(pre)
        out_ref[s] = (pre * sig).astype(BF)
        dy = jnp.where(full, dy_v[s].astype(F32), 0.0)
        pg = dy * sig * (1.0 + pre * (1.0 - sig))
        pg_v[s] = pg
        scaled = gain * pg
        gu_buf[4 * cap + s] = scaled.reshape(8, 8, 8, C).astype(BF)
        s_v[:, s * V:(s + 1) * V] = scaled.T.astype(BF)
        gain_sum = gain_sum + jnp.sum(pg * c_out, axis=0, keepdims=True)

    u_src = gu_buf.at[own]
    halo_start(u_src, gu_buf, us_sem, ur_sem)

    last = 27 * C
    rest = plan.rows - last
    if rest:
        acc[last:] = jnp.zeros((rest, C), F32)
        send[last:] = jnp.zeros((rest, C), BF)

    base = [[jnp.int32(st["start"])] for st in plan.streams]

    def rows_at(offset, n):
        return pl.ds(pl.multiple_of(offset, TILE), n)

    def scatter(t, p):
        ph = plan.streams[t]["phases"][p]
        r = plan.rank(ph["name"], i, j)
        copies = []
        for d in range(1, ph["g"]):
            q = lax.rem(r + d, ph["g"])
            copies.append(pltpu.make_async_remote_copy(
                src_ref=send.at[rows_at(base[t][p] + q * ph["n"], ph["n"])],
                dst_ref=recv.at[pl.ds(ph["room"] + (d - 1) * ph["n"], ph["n"])],
                send_sem=rs_s.at[ph["slot"] + d - 1], recv_sem=rs_r.at[ph["slot"] + d - 1],
                device_id=plan.peer(ph["name"], i, j, q), device_id_type=MESH))
        for c in copies:
            c.start()
        return copies

    def gather(t, p):
        ph = plan.streams[t]["phases"][p]
        r = plan.rank(ph["name"], i, j)
        mine = rows_at(base[t][p] + r * ph["n"], ph["n"])
        copies = []
        for d in range(1, ph["g"]):
            q = lax.rem(r + d, ph["g"])
            copies.append(pltpu.make_async_remote_copy(
                src_ref=whole.at[mine], dst_ref=whole.at[mine],
                send_sem=ag_s.at[ph["slot"] + d - 1], recv_sem=ag_r.at[ph["slot"] + d - 1],
                device_id=plan.peer(ph["name"], i, j, q), device_id_type=MESH))
        for c in copies:
            c.start()
        return copies

    def reduce(t, p, copies):
        phases = plan.streams[t]["phases"]
        ph = phases[p]
        r = plan.rank(ph["name"], i, j)
        for c in copies:
            c.wait()
        here = base[t][p] + r * ph["n"]
        base[t].append(here)
        mine = rows_at(here, ph["n"])
        value = acc[mine]
        for d in range(1, ph["g"]):
            value = value + recv[pl.ds(ph["room"] + (d - 1) * ph["n"], ph["n"])].astype(F32)
        if p + 1 < len(phases):
            acc[mine] = value
            send[mine] = value.astype(BF)
        else:
            whole[mine] = value.astype(BF)

    def advance(pending, p):
        for t, st in enumerate(plan.streams):
            steps = len(st["phases"])
            if p < steps:
                reduce(t, p, pending[t])
            else:
                for c in pending[t] or ():
                    c.wait()
            if p + 1 < steps:
                pending[t] = scatter(t, p + 1)
            elif 2 * steps - p - 2 >= 0:
                pending[t] = gather(t, 2 * steps - p - 2)
            else:
                pending[t] = None

    starts = [sum(g for _, g in plan.groups[:h]) for h in range(len(plan.groups))]

    def gain_send(h, value):
        name, g = plan.groups[h]
        r = plan.rank(name, i, j)
        gbuf[starts[h] + r] = jnp.broadcast_to(value, (8, C))
        copies = []
        for d in range(1, g):
            copies.append(pltpu.make_async_remote_copy(
                src_ref=gbuf.at[starts[h] + r], dst_ref=gbuf.at[starts[h] + r],
                send_sem=g_s.at[starts[h] + d], recv_sem=g_r.at[starts[h] + d],
                device_id=plan.peer(name, i, j, lax.rem(r + d, g)), device_id_type=MESH))
        for c in copies:
            c.start()
        return copies

    def gain_sum_of(h, copies):
        for c in copies:
            c.wait()
        value = gbuf[starts[h]]
        for q in range(1, plan.groups[h][1]):
            value = value + gbuf[starts[h] + q]
        return value

    pending = [None] * len(plan.streams)
    for m in range(9):
        total = None
        for s in range(cap):
            term = jnp.dot(s_v[:, s * V:(s + 1) * V], window(s, m // 3 - 1, m % 3 - 1), preferred_element_type=F32)
            total = term if total is None else total + term
        rows = slice(m * 3 * C, (m + 1) * 3 * C)
        value = total.T
        acc[rows] = value
        send[rows] = value.astype(BF)
        for t, st in enumerate(plan.streams):
            stop = st["start"] + st["rows"]
            if pending[t] is None and (stop <= (m + 1) * 3 * C or m == 8):
                pending[t] = scatter(t, 0)
    value = gain_sum
    flight = gain_send(0, value) if plan.groups else None
    advance(pending, 0)
    for h in range(1, len(plan.groups)):
        if h == 1:
            value = gain_sum_of(0, flight)
            flight = gain_send(1, value)
    halo_wait(u_src, gu_buf, us_sem, ur_sem)
    build(gu_buf)
    for s in range(cap):
        grad_ref[s] = (pg_v[s] + conv(s, wt_v)).astype(BF)
    steps = max(len(st["phases"]) for st in plan.streams)
    for p in range(1, 2 * steps):
        advance(pending, p)
        if p < len(plan.groups):
            value = gain_sum_of(p, flight)
            if p + 1 < len(plan.groups):
                flight = gain_send(p + 1, value)
    gsum_ref[...] = value
    sum_ref[...] = whole[0:27 * C]


def finish(out_ref, grad_ref, sum_ref, gsum_ref, out_hbm, grad_hbm, sum_hbm, gsum_out, wide, sems):
    copies = [pltpu.make_async_copy(out_ref, out_hbm, sems.at[0]),
              pltpu.make_async_copy(grad_ref, grad_hbm, sems.at[1])]
    for c in copies:
        c.start()
    n = wide.shape[0] // 9
    for m in range(9):
        rows = pl.ds(m * n, n)
        wide[rows] = sum_ref[rows].astype(F32)
        copies.append(pltpu.make_async_copy(wide.at[rows], sum_hbm.at[rows], sems.at[2 + m]))
        copies[-1].start()
    gsum_out[...] = gsum_ref[0:1]
    for c in copies:
        c.wait()


def on_device(gx, gy, features, cotangent, neighbours, weights, channel_gain):
    cap, C = features.shape[2], features.shape[-1]
    plan = Plan(gx, gy, 27 * C)
    V = 512
    hbm = pl.BlockSpec(memory_space=pl.ANY)
    far = pl.BlockSpec(memory_space=pltpu.HBM)
    vmem = pl.BlockSpec(memory_space=pltpu.VMEM)
    dma = pltpu.SemaphoreType.DMA
    parts = pl.pallas_call(
        partial(kernel, plan, gx, gy, cap, C),
        out_shape=(
            pltpu.VMEM((cap, V, C), BF),
            pltpu.VMEM((cap, V, C), BF),
            pltpu.VMEM((27 * C, C), BF),
            pltpu.VMEM((8, C), F32),
        ),
        in_specs=[pl.BlockSpec(memory_space=pltpu.SMEM), far, far, far, vmem],
        out_specs=(vmem, vmem, vmem, vmem),
        scratch_shapes=[
            pltpu.VMEM((9 * cap, 8, 8, 8, C), BF),
            pltpu.VMEM((9 * cap, 8, 8, 8, C), BF),
            pltpu.VMEM((cap, 10, 5, 16, 3 * C), BF),
            pltpu.VMEM((cap, 10, 4, 16, 3 * C), BF),
            pltpu.VMEM((27, C, C), BF),
            pltpu.VMEM((27, C, C), BF),
            pltpu.VMEM((cap, V, C), BF),
            pltpu.VMEM((cap, V, C), F32),
            pltpu.VMEM((C, cap * V), BF),
            pltpu.VMEM((plan.rows, C), F32),
            pltpu.VMEM((plan.rows, C), BF),
            pltpu.VMEM((plan.room, C), BF),
            pltpu.VMEM((plan.rows, C), BF),
            pltpu.VMEM((plan.members, 8, C), F32),
            dma((3,)), dma((8,)), dma((8,)), dma((8,)), dma((8,)),
            dma((plan.slots,)), dma((plan.slots,)), dma((plan.slots,)), dma((plan.slots,)),
            dma((plan.members,)), dma((plan.members,)),
        ],
        compiler_params=pltpu.CompilerParams(
            collective_id=0, has_side_effects=True, vmem_limit_bytes=62 * 1024 * 1024),
    )(
        neighbours.reshape(cap, 27),
        features.reshape(cap, 8, 8, 8, C),
        cotangent.reshape(cap, V, C),
        weights,
        channel_gain.reshape(1, C),
    )
    shape = (1, 1, cap, V, C)
    out, grad, weight_grad, gain_grad = pl.pallas_call(
        finish,
        out_shape=(
            jax.ShapeDtypeStruct((cap, V, C), BF),
            jax.ShapeDtypeStruct((cap, V, C), BF),
            jax.ShapeDtypeStruct((27 * C, C), F32),
            jax.ShapeDtypeStruct((1, C), F32),
        ),
        in_specs=[vmem] * 4,
        out_specs=(hbm, hbm, hbm, vmem),
        scratch_shapes=[pltpu.VMEM((27 * C, C), F32), dma((11,))],
        compiler_params=pltpu.CompilerParams(vmem_limit_bytes=16 * 1024 * 1024),
    )(*parts)
    return out.reshape(shape), grad.reshape(shape), weight_grad.reshape(27, C, C), gain_grad.reshape(C)


def solution(mesh):
    spec = P("gx", "gy", None, None, None)
    return jax.shard_map(
        partial(on_device, mesh.shape["gx"], mesh.shape["gy"]),
        mesh=mesh,
        in_specs=(spec, spec, P("gx", "gy", None, None), P(), P()),
        out_specs=(spec, spec, P(), P()),
        check_vma=False,
    )
```

```python
from functools import partial

import jax
import jax.numpy as jnp
from jax import lax
from jax.experimental import pallas as pl
from jax.experimental.pallas import tpu as pltpu
from jax.sharding import PartitionSpec as P

MESH = pl.DeviceIdType.MESH
BF = jnp.bfloat16
F32 = jnp.float32
ORDERS = (("core", "low", "high"), ("core", "low", "high"), ("core", "high", "low"), ("core", "high", "low"))
CUTS = (0, 3, 5, 6, 7)
SIDES = [(a, b) for a in (-1, 0, 1) for b in (-1, 0, 1) if (a, b) != (0, 0)]
TILE = 16


class Plan:
    def __init__(self, gx, gy, rows):
        low = 4 if gx % 4 == 0 else 1
        groups = {"core": gy, "low": low, "high": gx // low}
        self.low = low
        unit = gx * gy * TILE
        units = -(-rows // unit)
        cuts = [units * part // 7 for part in CUTS]
        self.rows = units * unit
        self.streams = []
        slot = 0
        room = 0
        for start, stop, order in zip(cuts[:-1], cuts[1:], ORDERS):
            count = stop - start
            if count == 0:
                continue
            phases = []
            size = count * unit
            for name in order:
                g = groups[name]
                if g == 1:
                    continue
                size //= g
                phases.append(dict(name=name, g=g, n=size, slot=slot, room=room))
                slot += g - 1
                room += (g - 1) * size
            self.streams.append(dict(start=start * unit, rows=count * unit, phases=phases))
        self.slots = slot
        self.room = room
        self.groups = [(name, g) for name, g in groups.items() if g > 1]
        self.members = sum(g for _, g in self.groups)

    def rank(self, name, i, j):
        if name == "core":
            return j
        return lax.rem(i, self.low) if name == "low" else i // self.low

    def peer(self, name, i, j, q):
        if name == "core":
            return (i, q)
        if name == "low":
            return (i - lax.rem(i, self.low) + q, j)
        return (q * self.low + lax.rem(i, self.low), j)


def face(d):
    return slice(0, 8) if d == 0 else (slice(7, 8) if d > 0 else slice(0, 1))


def rim(d):
    return slice(0, 8) if d == 0 else (slice(7, 8) if d < 0 else slice(0, 1))


def kernel(plan, gx, gy, cap, C,
           codes, x_hbm, dy_hbm, w_hbm, gain_ref,
           out_ref, grad_ref, sum_ref, gsum_ref,
           gx_buf, gu_buf, even, odd, w_v, wt_v, dy_v, pg_v, s_v, acc, send, recv, whole, gbuf,
           in_sem, xs_sem, xr_sem, us_sem, ur_sem, rs_s, rs_r, ag_s, ag_r, g_s, g_r):
    i = lax.axis_index("gx")
    j = lax.axis_index("gy")
    V = 512

    def inside(a, b):
        ok = None
        for t in ([i + a >= 0] if a < 0 else []) + ([i + a < gx] if a > 0 else []) + (
                [j + b >= 0] if b < 0 else []) + ([j + b < gy] if b > 0 else []):
            ok = t if ok is None else jnp.logical_and(ok, t)
        return ok

    own = pl.ds(4 * cap, cap)
    load_x = pltpu.make_async_copy(x_hbm, gx_buf.at[own], in_sem.at[0])
    load_w = pltpu.make_async_copy(w_hbm, w_v, in_sem.at[1])
    load_dy = pltpu.make_async_copy(dy_hbm, dy_v, in_sem.at[2])
    load_x.start()
    load_w.start()
    load_dy.start()

    barrier = pltpu.get_barrier_semaphore()
    count = jnp.int32(sum(g - 1 for _, g in plan.groups))
    for a, b in SIDES:
        ok = inside(a, b)
        count = count + ok.astype(jnp.int32)

        @pl.when(ok)
        def _():
            pl.semaphore_signal(barrier, inc=1, device_id=(i + a, j + b), device_id_type=MESH)

    for name, g in plan.groups:
        r = plan.rank(name, i, j)
        for d in range(1, g):
            pl.semaphore_signal(barrier, inc=1, device_id=plan.peer(name, i, j, lax.rem(r + d, g)),
                                device_id_type=MESH)
    pl.semaphore_wait(barrier, count)

    def halo(src, buf, ssem, rsem, m):
        a, b = SIDES[m]
        back = pl.ds((3 * (1 - a) + (1 - b)) * cap, cap)
        return pltpu.make_async_remote_copy(
            src_ref=src.at[:, face(a), face(b)], dst_ref=buf.at[back, face(a), face(b)],
            send_sem=ssem.at[m], recv_sem=rsem.at[m], device_id=(i + a, j + b), device_id_type=MESH)

    def halo_start(src, buf, ssem, rsem):
        for m, (a, b) in enumerate(SIDES):
            @pl.when(inside(a, b))
            def _():
                halo(src, buf, ssem, rsem, m).start()

    def halo_wait(src, buf, ssem, rsem):
        for m, (a, b) in enumerate(SIDES):
            @pl.when(inside(-a, -b))
            def _():
                halo(src, buf, ssem, rsem, m).wait_recv()

            @pl.when(inside(a, b))
            def _():
                halo(src, buf, ssem, rsem, m).wait_send()

    halo_start(x_hbm, gx_buf, xs_sem, xr_sem)

    load_w.wait()
    for k in range(27):
        wt_v[k] = w_v[26 - k].astype(F32).T.astype(BF)
    load_x.wait()
    load_dy.wait()
    halo_wait(x_hbm, gx_buf, xs_sem, xr_sem)

    def piece(buf, s, x, a, b, c):
        k = 9 * (a + 1) + 3 * (b + 1) + (c + 1)
        code = codes[s, k]
        if k == 13:
            value = buf[4 * cap + s, x]
        else:
            value = buf[jnp.maximum(code, 0), x, rim(b)]
        value = value.astype(F32)
        return jnp.where(jnp.full(value.shape, code, jnp.int32) >= 0, value, 0.0)

    def plane(buf, s, px, x, a):
        level = [jnp.concatenate([piece(buf, s, x, a, b, c) for b in (-1, 0, 1)], axis=0) for c in (-1, 0, 1)]
        z = lax.broadcasted_iota(jnp.int32, level[1].shape, 1)
        down = pltpu.roll(jnp.where(z == 7, level[0], level[1]), 1, 1)
        up = pltpu.roll(jnp.where(z == 0, level[2], level[1]), 7, 1)
        for c, value in enumerate((down, level[1], up)):
            lanes = slice(c * C, (c + 1) * C)
            even[s, px, :, :, lanes] = value.reshape(80, C).astype(BF).reshape(5, 16, C)
            odd[s, px, :, :, lanes] = value[1:9].reshape(64, C).astype(BF).reshape(4, 16, C)

    def build(buf):
        for s in range(cap):
            plane(buf, s, 0, 7, -1)

            @pl.loop(0, 8)
            def _(x):
                plane(buf, s, x + 1, x, 0)

            plane(buf, s, 9, 0, 1)

    def window(s, a, b):
        xs = slice(1 + a, 9 + a)
        if b == 0:
            return odd[s, xs].reshape(V, 3 * C)
        return (even[s, xs, 0:4] if b < 0 else even[s, xs, 1:5]).reshape(V, 3 * C)

    def conv(s, w):
        total = None
        for m in range(9):
            term = jnp.dot(window(s, m // 3 - 1, m % 3 - 1), w[3 * m:3 * m + 3].reshape(3 * C, C),
                           preferred_element_type=F32)
            total = term if total is None else total + term
        return total

    build(gx_buf)
    gain = gain_ref[...]
    gain_sum = jnp.zeros((1, C), F32)
    for s in range(cap):
        c_out = conv(s, w_v)
        full = jnp.full((V, C), codes[s, 13], jnp.int32) >= 0
        mx = jnp.where(full, gx_buf[4 * cap + s].astype(F32).reshape(V, C), 0.0)
        pre = mx + gain * c_out
        sig = jax.nn.sigmoid(pre)
        out_ref[s] = (pre * sig).astype(BF)
        dy = jnp.where(full, dy_v[s].astype(F32), 0.0)
        pg = dy * sig * (1.0 + pre * (1.0 - sig))
        pg_v[s] = pg
        scaled = gain * pg
        gu_buf[4 * cap + s] = scaled.reshape(8, 8, 8, C).astype(BF)
        s_v[:, s * V:(s + 1) * V] = scaled.T.astype(BF)
        gain_sum = gain_sum + jnp.sum(pg * c_out, axis=0, keepdims=True)

    u_src = gu_buf.at[own]
    halo_start(u_src, gu_buf, us_sem, ur_sem)

    last = 27 * C
    rest = plan.rows - last
    if rest:
        acc[last:] = jnp.zeros((rest, C), F32)
        send[last:] = jnp.zeros((rest, C), BF)

    base = [[jnp.int32(st["start"])] for st in plan.streams]

    def rows_at(offset, n):
        return pl.ds(pl.multiple_of(offset, TILE), n)

    def scatter(t, p):
        ph = plan.streams[t]["phases"][p]
        r = plan.rank(ph["name"], i, j)
        copies = []
        for d in range(1, ph["g"]):
            q = lax.rem(r + d, ph["g"])
            copies.append(pltpu.make_async_remote_copy(
                src_ref=send.at[rows_at(base[t][p] + q * ph["n"], ph["n"])],
                dst_ref=recv.at[pl.ds(ph["room"] + (d - 1) * ph["n"], ph["n"])],
                send_sem=rs_s.at[ph["slot"] + d - 1], recv_sem=rs_r.at[ph["slot"] + d - 1],
                device_id=plan.peer(ph["name"], i, j, q), device_id_type=MESH))
        for c in copies:
            c.start()
        return copies

    def gather(t, p):
        ph = plan.streams[t]["phases"][p]
        r = plan.rank(ph["name"], i, j)
        mine = rows_at(base[t][p] + r * ph["n"], ph["n"])
        copies = []
        for d in range(1, ph["g"]):
            q = lax.rem(r + d, ph["g"])
            copies.append(pltpu.make_async_remote_copy(
                src_ref=whole.at[mine], dst_ref=whole.at[mine],
                send_sem=ag_s.at[ph["slot"] + d - 1], recv_sem=ag_r.at[ph["slot"] + d - 1],
                device_id=plan.peer(ph["name"], i, j, q), device_id_type=MESH))
        for c in copies:
            c.start()
        return copies

    def reduce(t, p, copies):
        phases = plan.streams[t]["phases"]
        ph = phases[p]
        r = plan.rank(ph["name"], i, j)
        for c in copies:
            c.wait()
        here = base[t][p] + r * ph["n"]
        base[t].append(here)
        mine = rows_at(here, ph["n"])
        value = acc[mine]
        for d in range(1, ph["g"]):
            value = value + recv[pl.ds(ph["room"] + (d - 1) * ph["n"], ph["n"])].astype(F32)
        if p + 1 < len(phases):
            acc[mine] = value
            send[mine] = value.astype(BF)
        else:
            whole[mine] = value.astype(BF)

    def advance(pending, p):
        for t, st in enumerate(plan.streams):
            steps = len(st["phases"])
            if p < steps:
                reduce(t, p, pending[t])
            else:
                for c in pending[t] or ():
                    c.wait()
            if p + 1 < steps:
                pending[t] = scatter(t, p + 1)
            elif 2 * steps - p - 2 >= 0:
                pending[t] = gather(t, 2 * steps - p - 2)
            else:
                pending[t] = None

    starts = [sum(g for _, g in plan.groups[:h]) for h in range(len(plan.groups))]

    def gain_send(h, value):
        name, g = plan.groups[h]
        r = plan.rank(name, i, j)
        gbuf[starts[h] + r] = jnp.broadcast_to(value, (8, C))
        copies = []
        for d in range(1, g):
            copies.append(pltpu.make_async_remote_copy(
                src_ref=gbuf.at[starts[h] + r], dst_ref=gbuf.at[starts[h] + r],
                send_sem=g_s.at[starts[h] + d], recv_sem=g_r.at[starts[h] + d],
                device_id=plan.peer(name, i, j, lax.rem(r + d, g)), device_id_type=MESH))
        for c in copies:
            c.start()
        return copies

    def gain_sum_of(h, copies):
        for c in copies:
            c.wait()
        value = gbuf[starts[h]]
        for q in range(1, plan.groups[h][1]):
            value = value + gbuf[starts[h] + q]
        return value

    pending = [None] * len(plan.streams)
    for m in range(9):
        total = None
        for s in range(cap):
            term = jnp.dot(s_v[:, s * V:(s + 1) * V], window(s, m // 3 - 1, m % 3 - 1), preferred_element_type=F32)
            total = term if total is None else total + term
        rows = slice(m * 3 * C, (m + 1) * 3 * C)
        value = total.T
        acc[rows] = value
        send[rows] = value.astype(BF)
        for t, st in enumerate(plan.streams):
            stop = st["start"] + st["rows"]
            if pending[t] is None and (stop <= (m + 1) * 3 * C or m == 8):
                pending[t] = scatter(t, 0)
    value = gain_sum
    flight = gain_send(0, value) if plan.groups else None
    advance(pending, 0)
    for h in range(1, len(plan.groups)):
        if h == 1:
            value = gain_sum_of(0, flight)
            flight = gain_send(1, value)
    halo_wait(u_src, gu_buf, us_sem, ur_sem)
    build(gu_buf)
    for s in range(cap):
        grad_ref[s] = (pg_v[s] + conv(s, wt_v)).astype(BF)
    steps = max(len(st["phases"]) for st in plan.streams)
    for p in range(1, 2 * steps):
        advance(pending, p)
        if p < len(plan.groups):
            value = gain_sum_of(p, flight)
            if p + 1 < len(plan.groups):
                flight = gain_send(p + 1, value)
    gsum_ref[...] = value
    sum_ref[...] = whole[0:27 * C]


def finish(out_ref, grad_ref, sum_ref, gsum_ref, out_hbm, grad_hbm, sum_hbm, gsum_out, wide, sems):
    copies = [pltpu.make_async_copy(out_ref, out_hbm, sems.at[0]),
              pltpu.make_async_copy(grad_ref, grad_hbm, sems.at[1])]
    for c in copies:
        c.start()
    n = wide.shape[0] // 9
    for m in range(9):
        rows = pl.ds(m * n, n)
        wide[rows] = sum_ref[rows].astype(F32)
        copies.append(pltpu.make_async_copy(wide.at[rows], sum_hbm.at[rows], sems.at[2 + m]))
        copies[-1].start()
    gsum_out[...] = gsum_ref[0:1]
    for c in copies:
        c.wait()


def on_device(gx, gy, features, cotangent, neighbours, weights, channel_gain):
    cap, C = features.shape[2], features.shape[-1]
    plan = Plan(gx, gy, 27 * C)
    V = 512
    hbm = pl.BlockSpec(memory_space=pl.ANY)
    far = pl.BlockSpec(memory_space=pltpu.HBM)
    vmem = pl.BlockSpec(memory_space=pltpu.VMEM)
    dma = pltpu.SemaphoreType.DMA
    parts = pl.pallas_call(
        partial(kernel, plan, gx, gy, cap, C),
        out_shape=(
            pltpu.VMEM((cap, V, C), BF),
            pltpu.VMEM((cap, V, C), BF),
            pltpu.VMEM((27 * C, C), BF),
            pltpu.VMEM((8, C), F32),
        ),
        in_specs=[pl.BlockSpec(memory_space=pltpu.SMEM), far, far, far, vmem],
        out_specs=(vmem, vmem, vmem, vmem),
        scratch_shapes=[
            pltpu.VMEM((9 * cap, 8, 8, 8, C), BF),
            pltpu.VMEM((9 * cap, 8, 8, 8, C), BF),
            pltpu.VMEM((cap, 10, 5, 16, 3 * C), BF),
            pltpu.VMEM((cap, 10, 4, 16, 3 * C), BF),
            pltpu.VMEM((27, C, C), BF),
            pltpu.VMEM((27, C, C), BF),
            pltpu.VMEM((cap, V, C), BF),
            pltpu.VMEM((cap, V, C), F32),
            pltpu.VMEM((C, cap * V), BF),
            pltpu.VMEM((plan.rows, C), F32),
            pltpu.VMEM((plan.rows, C), BF),
            pltpu.VMEM((plan.room, C), BF),
            pltpu.VMEM((plan.rows, C), BF),
            pltpu.VMEM((plan.members, 8, C), F32),
            dma((3,)), dma((8,)), dma((8,)), dma((8,)), dma((8,)),
            dma((plan.slots,)), dma((plan.slots,)), dma((plan.slots,)), dma((plan.slots,)),
            dma((plan.members,)), dma((plan.members,)),
        ],
        compiler_params=pltpu.CompilerParams(
            collective_id=0, has_side_effects=True, vmem_limit_bytes=62 * 1024 * 1024),
    )(
        neighbours.reshape(cap, 27),
        features.reshape(cap, 8, 8, 8, C),
        cotangent.reshape(cap, V, C),
        weights,
        channel_gain.reshape(1, C),
    )
    shape = (1, 1, cap, V, C)
    out, grad, weight_grad, gain_grad = pl.pallas_call(
        finish,
        out_shape=(
            jax.ShapeDtypeStruct((cap, V, C), BF),
            jax.ShapeDtypeStruct((cap, V, C), BF),
            jax.ShapeDtypeStruct((27 * C, C), F32),
            jax.ShapeDtypeStruct((1, C), F32),
        ),
        in_specs=[vmem] * 4,
        out_specs=(hbm, hbm, hbm, vmem),
        scratch_shapes=[pltpu.VMEM((27 * C, C), F32), dma((11,))],
        compiler_params=pltpu.CompilerParams(vmem_limit_bytes=16 * 1024 * 1024),
    )(*parts)
    return out.reshape(shape), grad.reshape(shape), weight_grad.reshape(27, C, C), gain_grad.reshape(C)


def solution(mesh):
    spec = P("gx", "gy", None, None, None)
    return jax.shard_map(
        partial(on_device, mesh.shape["gx"], mesh.shape["gy"]),
        mesh=mesh,
        in_specs=(spec, spec, P("gx", "gy", None, None), P(), P()),
        out_specs=(spec, spec, P(), P()),
        check_vma=False,
    )
```
